32 devices in a mesh: ka: 4 (over y, x), rp: 8 (over z, core).
Axes of the slice: x: 2, y: 2, z: 4, core: 2. Of those that a mesh axis runs over, the one named last changes fastest.
Arguments:
- coupling_table: bfloat16 [512, 256, 1024], P('ka', 'rp'), may hold values from -0.016479492 to 0.016479492
- k_points: int32 [3, 2048], P(None, 'ka'), may hold values from 0 to 15
- re_vectors: int32 [3, 512], replicated, may hold values from -6 to 6
- rp_vectors: int32 [3, 256], P(None, 'rp'), may hold values from -6 to 6
- q_points: int32 [3, 2], replicated, may hold values from 0 to 15
Outputs:
- bloch_coupling: float32 [2048, 2048], P(('ka', 'rp'))
The draws below stay inside these ranges and needn't reach their ends.
All inputs are finite; a program needn't handle non-finite values.
Results may differ from the reference program's by a relative error of at most 0.0022.
Values may be sent and summed in bfloat16 or wider, within the bound.
A program may use at most 64 MiB of HBM per device.

```python
import math
import jax
import jax.numpy as jnp
from jax import lax

RE = 512
RP = 256
M = 512
Q = 2
NKG = 16
KTOT = 2048


def place_ends(values, rng, smallest, high):
    index_at = [jax.random.randint(jax.random.fold_in(rng, axis), (), 0, length) for axis, length in enumerate(values.shape)]
    main_axis = values.shape.index(max(values.shape))
    neighbour = index_at[:main_axis] + [(index_at[main_axis] + 1) % values.shape[main_axis]] + index_at[main_axis + 1:]
    return values.at[tuple(index_at)].set(smallest).at[tuple(neighbour)].set(high)


def shard_levels(own_key, dims, cuts, smallest, largest):
    level = 1.0
    for position, parts in cuts:
        draws = jax.random.uniform(jax.random.fold_in(jax.random.fold_in(own_key, 6), position), (parts,), jnp.float32, smallest / len(cuts), largest / len(cuts))
        level = level * jnp.repeat(jnp.exp(draws), dims[position] // parts).reshape((-1,) + (1,) * (len(dims) - 1 - position))
    return level


def noise(rng, shape, scale, most, cuts=(), held_as=jnp.bfloat16):
    result = jax.random.normal(rng, shape, jnp.float32) * scale
    if len(cuts) > 0:
        result = shard_levels(rng, shape, cuts, -0.22, 0.18) * result
    return jnp.clip(result, min=-most, max=most).astype(held_as)


def setup_inputs(seed: int = 0) -> dict:
    streams_of = jax.random.split(jax.random.key(seed), 6)
    coupling_table = noise(streams_of[0], (RE, RP, 2 * M), 0.00275, 0.016479492, ((0, 4), (1, 8)))
    k_points = place_ends(jax.random.randint(streams_of[1], (3, KTOT), 0, NKG), jax.random.fold_in(streams_of[1], 1), 0, NKG - 1).astype(jnp.int32)
    re_vectors = place_ends(jax.random.randint(streams_of[2], (3, RE), -6, 7), jax.random.fold_in(streams_of[2], 1), -6, 6).astype(jnp.int32)
    rp_vectors = place_ends(jax.random.randint(streams_of[3], (3, RP), -6, 7), jax.random.fold_in(streams_of[3], 1), -6, 6).astype(jnp.int32)
    q_points = place_ends(jax.random.randint(streams_of[4], (3, Q), 0, NKG), jax.random.fold_in(streams_of[4], 1), 0, NKG - 1).astype(jnp.int32)
    return dict(coupling_table=coupling_table, k_points=k_points, re_vectors=re_vectors, rp_vectors=rp_vectors, q_points=q_points)


def phases(left, right):
    nested = left[0][:, None] * right[0][None, :] + left[1][:, None] * right[1][None, :] + left[2][:, None] * right[2][None, :]
    wrapped = jnp.mod(nested, NKG).astype(jnp.int32)
    angles = wrapped.astype(jnp.float32) * (2.0 * math.pi / NKG)
    return jnp.cos(angles), jnp.sin(angles)


def reference(coupling_table, k_points, re_vectors, rp_vectors, q_points):
    high = lax.Precision.HIGHEST
    q_cos, q_sin = phases(q_points, rp_vectors)
    values = coupling_table.astype(jnp.float32).reshape(RE, RP, 2, M)
    real_in = values[:, :, 0, :]
    imag_in = values[:, :, 1, :]
    real_mid = jnp.einsum("qr,erm->eqm", q_cos, real_in, precision=high) - jnp.einsum("qr,erm->eqm", q_sin, imag_in, precision=high)
    imag_mid = jnp.einsum("qr,erm->eqm", q_sin, real_in, precision=high) + jnp.einsum("qr,erm->eqm", q_cos, imag_in, precision=high)
    real_mid = real_mid.reshape(RE, Q * M)
    imag_mid = imag_mid.reshape(RE, Q * M)
    k_cos, k_sin = phases(k_points, re_vectors)
    k_cos = k_cos.astype(jnp.bfloat16).astype(jnp.float32)
    k_sin = k_sin.astype(jnp.bfloat16).astype(jnp.float32)
    real_out = jnp.dot(k_cos, real_mid, precision=high, preferred_element_type=jnp.float32) - jnp.dot(k_sin, imag_mid, precision=high, preferred_element_type=jnp.float32)
    imag_out = jnp.dot(k_sin, real_mid, precision=high, preferred_element_type=jnp.float32) + jnp.dot(k_cos, imag_mid, precision=high, preferred_element_type=jnp.float32)
    return jnp.stack([real_out, imag_out], axis=1).reshape(KTOT, 2 * Q * M)
```

```python
import functools
import math

import jax
import jax.numpy as jnp
import numpy as np
from jax import lax
from jax.experimental import pallas as pl
from jax.experimental.pallas import tpu as pltpu
from jax.sharding import PartitionSpec as P

NKG = 16
MESH = pl.DeviceIdType.MESH
GROUP = 8
CHUNK = 32

_B = np.arange(1.0, 5.0)
SINE = [
    float(c)
    for c in np.linalg.solve(
        _B[:, None] ** np.arange(1.0, 8.0, 2.0)[None, :], np.sin(_B * 2.0 * math.pi / NKG)
    )
]


def grid_sin(b):
    s = b * b
    return b * (SINE[0] + s * (SINE[1] + s * (SINE[2] + s * SINE[3])))


def grid_phases(n):
    n = n - NKG * jnp.floor(n * (1.0 / NKG))
    m = n - 4.0
    m = jnp.where(m < 0.0, m + NKG, m)
    return grid_sin(jnp.abs(n - 8.0) - 4.0), grid_sin(jnp.abs(m - 8.0) - 4.0)


def kernel(
    sizes, q_ref, k_ref, re_ref, rp_ref, table_ref, out_ref,
    table, lhs, partial, pair_in, z_out, z_in, frag, kn, kph, own, out_send, out_in,
    table_sem, pair_s, pair_r, z_s, z_r, ka_s, ka_r, o_s, o_r,
):
    n_ka, n_rp, E, R, M, Q, KL = sizes
    nz = n_rp // 2
    C = Q * M // n_rp
    Ec = min(CHUNK, E)
    NC = E // Ec
    ka = lax.axis_index("ka")
    me = lax.axis_index("rp")
    par = lax.rem(me, 2)
    zi = me // 2
    f32, bf16 = jnp.float32, jnp.bfloat16

    loads = []
    for c in range(NC):
        cp = pltpu.make_async_copy(
            table_ref.at[pl.ds(c * Ec * R, Ec * R)], table.at[pl.ds(c * Ec * R, Ec * R)],
            table_sem.at[c],
        )
        cp.start()
        loads.append(cp)

    barrier = pltpu.get_barrier_semaphore()
    for d in range(1, n_rp):
        pl.semaphore_signal(
            barrier, inc=1, device_id={"rp": lax.rem(me + d, n_rp)}, device_id_type=MESH
        )
    for d in range(1, n_ka):
        pl.semaphore_signal(
            barrier, inc=1, device_id={"ka": lax.rem(ka + d, n_ka)}, device_id_type=MESH
        )

    K = GROUP * R
    lane = lax.broadcasted_iota(jnp.int32, (GROUP, K), 1)
    row = lax.broadcasted_iota(jnp.int32, (GROUP, K), 0)
    keep = (lane >= row * R) & (lane < row * R + R)
    tiled = [jnp.concatenate([rp_ref[i : i + 1, :]] * GROUP, axis=1) for i in range(3)]
    parts = [[], []]
    for q in range(Q):
        n = q_ref[0, q] * tiled[0] + q_ref[1, q] * tiled[1] + q_ref[2, q] * tiled[2]
        for side, x in enumerate(grid_phases(n.astype(f32))):
            parts[side].append(jnp.where(keep, jnp.broadcast_to(x, (GROUP, K)), 0.0))
    exact = jnp.concatenate(parts[0] + parts[1], axis=0)
    high = exact.astype(bf16)
    half = 2 * Q * GROUP
    lhs[0:half, :] = high
    lhs[half : 2 * half, :] = (exact - high.astype(f32)).astype(bf16)

    def pair_copy(c):
        rows = pl.ds(c * Ec, Ec)
        return pltpu.make_async_remote_copy(
            src_ref=partial.at[1 - par, :, rows, :], dst_ref=pair_in.at[:, rows, :],
            send_sem=pair_s.at[c], recv_sem=pair_r.at[c],
            device_id={"rp": me + 1 - 2 * par}, device_id_type=MESH,
        )

    def z_copy(c, d):
        return pltpu.make_async_remote_copy(
            src_ref=z_out.at[c, d - 1], dst_ref=z_in.at[c, d - 1],
            send_sem=z_s.at[c, d - 1], recv_sem=z_r.at[c, d - 1],
            device_id={"rp": lax.rem(zi + d, nz) * 2 + par}, device_id_type=MESH,
        )

    def ka_copy(c, d):
        piece = frag.at[:, ka, pl.ds(c * Ec, Ec), :]
        return pltpu.make_async_remote_copy(
            src_ref=piece, dst_ref=piece,
            send_sem=ka_s.at[c, d - 1], recv_sem=ka_r.at[c, d - 1],
            device_id={"ka": lax.rem(ka + d, n_ka)}, device_id_type=MESH,
        )

    def out_copy(d):
        dest = lax.rem(me + d, n_rp)
        return pltpu.make_async_remote_copy(
            src_ref=out_send.at[d - 1], dst_ref=out_in.at[d - 1],
            send_sem=o_s.at[d - 1], recv_sem=o_r.at[d - 1],
            device_id={"rp": dest}, device_id_type=MESH,
        )

    def mid_sums(c):
        loads[c].wait()
        for g in range(Ec // GROUP):
            e0 = c * Ec + g * GROUP
            prod = jnp.dot(lhs[...], table[pl.ds(e0 * R, K), :], preferred_element_type=f32)
            prod = prod[:half] + prod[half:]
            cos_p, sin_p = prod[: half // 2], prod[half // 2 :]
            real = cos_p[:, :M] - sin_p[:, M:]
            imag = sin_p[:, :M] + cos_p[:, M:]
            for p in range(n_rp):
                q, col = (p * C) // M, (p * C) % M
                pick = slice(q * GROUP, (q + 1) * GROUP)
                block = jnp.concatenate(
                    [real[pick, col : col + C], imag[pick, col : col + C]], axis=1
                )
                partial[p % 2, p // 2, e0 : e0 + GROUP, :] = block

    def to_owners(c):
        pair_copy(c).wait()
        rows = pl.ds(c * Ec, Ec)
        for d in range(1, nz):
            j = lax.rem(zi + d, nz)
            z_out[c, d - 1] = (partial[par, j, rows, :] + pair_in[j, rows, :]).astype(bf16)
            z_copy(c, d).start()

    def to_groups(c):
        rows = pl.ds(c * Ec, Ec)
        total = partial[par, zi, rows, :] + pair_in[zi, rows, :]
        for d in range(1, nz):
            z_copy(c, d).wait()
            total = total + z_in[c, d - 1].astype(f32)
        high = total.astype(bf16)
        frag[0, ka, rows, :] = high
        frag[1, ka, rows, :] = (total - high.astype(f32)).astype(bf16)
        for d in range(1, n_ka):
            ka_copy(c, d).start()

    def k_block(p):
        cos_k, sin_k = grid_phases(kn[p * KL : (p + 1) * KL, :])
        kph[p, 0:KL, :] = cos_k.astype(bf16)
        kph[p, KL : 2 * KL, :] = sin_k.astype(bf16)

    ticks = NC + 2
    done = 0
    for t in range(ticks):
        if t < NC:
            mid_sums(t)
            if t == 0:
                pl.semaphore_wait(barrier, n_rp + n_ka - 2)
            pair_copy(t).start()
        if t == 0:
            kn[...] = lax.dot_general(
                k_ref[...].astype(f32).astype(bf16), re_ref[...].astype(f32).astype(bf16),
                (((0,), (0,)), ((), ())), preferred_element_type=f32,
            )
        upto = n_rp * (t + 1) // ticks
        for p in range(done, upto):
            k_block(p)
        done = upto
        if 1 <= t <= NC:
            to_owners(t - 1)
        if 2 <= t:
            to_groups(t - 2)

    for c in range(NC):
        for d in range(1, n_ka):
            src = frag.at[:, lax.rem(ka + n_ka - d, n_ka), pl.ds(c * Ec, Ec), :]
            ka_copy(c, d).wait_send()
            pltpu.make_async_remote_copy(
                src_ref=src, dst_ref=src,
                send_sem=ka_s.at[c, d - 1], recv_sem=ka_r.at[c, d - 1],
                device_id={"ka": lax.rem(ka + d, n_ka)}, device_id_type=MESH,
            ).wait_recv()

    def coupling(dest):
        ph = kph[dest]
        mid = frag[...].reshape(2, n_ka * E, 2 * C)
        s = jnp.dot(ph, mid[0], preferred_element_type=f32)
        s = s + jnp.dot(ph, mid[1], preferred_element_type=f32)
        real = s[:KL, :C] - s[KL:, C:]
        imag = s[KL:, :C] + s[:KL, C:]
        return jnp.concatenate([real, imag], axis=1)

    for d in range(1, n_rp):
        out_send[d - 1] = coupling(lax.rem(me + d, n_rp)).astype(bf16)
        out_copy(d).start()
    own[...] = coupling(me)

    for d in range(1, n_rp):
        out_copy(d).wait()
    for s in range(n_rp):
        lo, hi = s * C, Q * M + s * C

        @pl.when(me == s)
        def _():
            out_ref[:, lo : lo + C] = own[:, :C]
            out_ref[:, hi : hi + C] = own[:, C:]

        @pl.when(me != s)
        def _():
            block = out_in[lax.rem(me - s + n_rp, n_rp) - 1].astype(f32)
            out_ref[:, lo : lo + C] = block[:, :C]
            out_ref[:, hi : hi + C] = block[:, C:]


def per_device(mesh, coupling_table, k_points, re_vectors, rp_vectors, q_points):
    n_ka, n_rp = mesh.shape["ka"], mesh.shape["rp"]
    E, R, width = coupling_table.shape
    M, Q = width // 2, q_points.shape[1]
    kt = k_points.shape[1]
    KL = kt // n_rp
    nz, C = n_rp // 2, Q * M // n_rp
    Ec = min(CHUNK, E)
    NC = E // Ec
    f32, bf16 = jnp.float32, jnp.bfloat16
    dma = pltpu.SemaphoreType.DMA
    vmem = pl.BlockSpec(memory_space=pltpu.VMEM)
    return pl.pallas_call(
        functools.partial(kernel, (n_ka, n_rp, E, R, M, Q, KL)),
        out_shape=jax.ShapeDtypeStruct((KL, 2 * Q * M), f32),
        in_specs=[
            pl.BlockSpec(memory_space=pltpu.SMEM), vmem, vmem, vmem,
            pl.BlockSpec(memory_space=pl.ANY),
        ],
        out_specs=vmem,
        scratch_shapes=[
            pltpu.VMEM((E * R, width), bf16),
            pltpu.VMEM((4 * Q * GROUP, GROUP * R), bf16),
            pltpu.VMEM((2, nz, E, 2 * C), f32),
            pltpu.VMEM((nz, E, 2 * C), f32),
            pltpu.VMEM((NC, nz - 1, Ec, 2 * C), bf16),
            pltpu.VMEM((NC, nz - 1, Ec, 2 * C), bf16),
            pltpu.VMEM((2, n_ka, E, 2 * C), bf16),
            pltpu.VMEM((kt, n_ka * E), f32),
            pltpu.VMEM((n_rp, 2 * KL, n_ka * E), bf16),
            pltpu.VMEM((KL, 2 * C), f32),
            pltpu.VMEM((n_rp - 1, KL, 2 * C), bf16),
            pltpu.VMEM((n_rp - 1, KL, 2 * C), bf16),
            dma((NC,)), dma((NC,)), dma((NC,)), dma((NC, nz - 1)), dma((NC, nz - 1)),
            dma((NC, n_ka - 1)), dma((NC, n_ka - 1)), dma((n_rp - 1,)), dma((n_rp - 1,)),
        ],
        compiler_params=pltpu.CompilerParams(
            collective_id=0, has_side_effects=True, vmem_limit_bytes=40 * 1024 * 1024
        ),
        name="interpolate",
    )(q_points, k_points, re_vectors, rp_vectors, coupling_table.reshape(E * R, width))


def solution(mesh):
    placed = (P("ka", "rp", None), P(None, "ka"), P(), P(None, "rp"), P())
    return jax.shard_map(
        functools.partial(per_device, mesh), mesh=mesh, in_specs=placed,
        out_specs=P(("ka", "rp"), None), check_vma=False,
    )
```

```python
import functools
import math

import jax
import jax.numpy as jnp
import numpy as np
from jax import lax
from jax.experimental import pallas as pl
from jax.experimental.pallas import tpu as pltpu
from jax.sharding import PartitionSpec as P

NKG = 16
MESH = pl.DeviceIdType.MESH
GROUP = 8
CHUNK = 32

LAG = 1

_B = np.arange(1.0, 5.0)
SINE = [
    float(c)
    for c in np.linalg.solve(
        _B[:, None] ** np.arange(1.0, 8.0, 2.0)[None, :], np.sin(_B * 2.0 * math.pi / NKG)
    )
]


def grid_sin(b):
    s = b * b
    return b * (SINE[0] + s * (SINE[1] + s * (SINE[2] + s * SINE[3])))


def grid_phases(n):
    n = n - NKG * jnp.floor(n * (1.0 / NKG))
    m = n - 4.0
    m = jnp.where(m < 0.0, m + NKG, m)
    return grid_sin(jnp.abs(n - 8.0) - 4.0), grid_sin(jnp.abs(m - 8.0) - 4.0)


def kernel(
    sizes, q_hbm, k_hbm, re_hbm, rp_hbm, table_ref, out_ref,
    q_ref, k_ref, re_ref, rp_ref, table, lhs, partial, pair_in, z_out, z_in, frag, kn, kph, own, out_send, out_in,
    small_sem, table_sem, pair_s, pair_r, z_s, z_r, ka_s, ka_r, o_s, o_r,
):
    n_ka, n_rp, E, R, M, Q, KL = sizes
    nz = n_rp // 2
    C = Q * M // n_rp
    Ec = min(CHUNK, E)
    NC = E // Ec
    ka = lax.axis_index("ka")
    me = lax.axis_index("rp")
    par = lax.rem(me, 2)
    zi = me // 2
    f32, bf16 = jnp.float32, jnp.bfloat16

    small = []
    for i, (src, dst) in enumerate(
        ((q_hbm, q_ref), (rp_hbm, rp_ref), (k_hbm, k_ref), (re_hbm, re_ref))
    ):
        cp = pltpu.make_async_copy(src, dst, small_sem.at[i])
        cp.start()
        small.append(cp)
    loads = []
    for c in range(NC):
        cp = pltpu.make_async_copy(
            table_ref.at[pl.ds(c * Ec * R, Ec * R)], table.at[pl.ds(c * Ec * R, Ec * R)],
            table_sem.at[c],
        )
        cp.start()
        loads.append(cp)

    barrier = pltpu.get_barrier_semaphore()
    for d in range(1, n_rp):
        pl.semaphore_signal(
            barrier, inc=1, device_id={"rp": lax.rem(me + d, n_rp)}, device_id_type=MESH
        )
    for d in range(1, n_ka):
        pl.semaphore_signal(
            barrier, inc=1, device_id={"ka": lax.rem(ka + d, n_ka)}, device_id_type=MESH
        )

    small[0].wait()
    small[1].wait()
    K = GROUP * R
    lane = lax.broadcasted_iota(jnp.int32, (GROUP, K), 1)
    row = lax.broadcasted_iota(jnp.int32, (GROUP, K), 0)
    keep = (lane >= row * R) & (lane < row * R + R)
    tiled = [jnp.concatenate([rp_ref[i : i + 1, :]] * GROUP, axis=1) for i in range(3)]
    parts = [[], []]
    for q in range(Q):
        n = sum(q_ref[q : q + 1, i : i + 1] * tiled[i] for i in range(3))
        for side, x in enumerate(grid_phases(n.astype(f32))):
            parts[side].append(jnp.where(keep, jnp.broadcast_to(x, (GROUP, K)), 0.0))
    exact = jnp.concatenate(parts[0] + parts[1], axis=0)
    high = exact.astype(bf16)
    half = 2 * Q * GROUP
    lhs[0:half, :] = high
    lhs[half : 2 * half, :] = (exact - high.astype(f32)).astype(bf16)

    def pair_copy(c):
        rows = pl.ds(c * Ec, Ec)
        return pltpu.make_async_remote_copy(
            src_ref=partial.at[1 - par, :, rows, :], dst_ref=pair_in.at[:, rows, :],
            send_sem=pair_s.at[c], recv_sem=pair_r.at[c],
            device_id={"rp": me + 1 - 2 * par}, device_id_type=MESH,
        )

    def z_copy(c, d):
        return pltpu.make_async_remote_copy(
            src_ref=z_out.at[c, d - 1], dst_ref=z_in.at[c, d - 1],
            send_sem=z_s.at[c, d - 1], recv_sem=z_r.at[c, d - 1],
            device_id={"rp": lax.rem(zi + d, nz) * 2 + par}, device_id_type=MESH,
        )

    def ka_copy(c, d):
        piece = frag.at[:, ka, pl.ds(c * Ec, Ec), :]
        return pltpu.make_async_remote_copy(
            src_ref=piece, dst_ref=piece,
            send_sem=ka_s.at[c, d - 1], recv_sem=ka_r.at[c, d - 1],
            device_id={"ka": lax.rem(ka + d, n_ka)}, device_id_type=MESH,
        )

    def out_copy(d):
        dest = lax.rem(me + d, n_rp)
        return pltpu.make_async_remote_copy(
            src_ref=out_send.at[d - 1], dst_ref=out_in.at[d - 1],
            send_sem=o_s.at[d - 1], recv_sem=o_r.at[d - 1],
            device_id={"rp": dest}, device_id_type=MESH,
        )

    def mid_sums(c):
        loads[c].wait()
        for g in range(Ec // GROUP):
            e0 = c * Ec + g * GROUP
            prod = jnp.dot(lhs[...], table[pl.ds(e0 * R, K), :], preferred_element_type=f32)
            prod = prod[:half] + prod[half:]
            cos_p, sin_p = prod[: half // 2], prod[half // 2 :]
            real = cos_p[:, :M] - sin_p[:, M:]
            imag = sin_p[:, :M] + cos_p[:, M:]
            for p in range(n_rp):
                q, col = (p * C) // M, (p * C) % M
                pick = slice(q * GROUP, (q + 1) * GROUP)
                block = jnp.concatenate(
                    [real[pick, col : col + C], imag[pick, col : col + C]], axis=1
                )
                partial[p % 2, p // 2, e0 : e0 + GROUP, :] = block

    def to_owners(c):
        pair_copy(c).wait()
        rows = pl.ds(c * Ec, Ec)
        for d in range(1, nz):
            j = lax.rem(zi + d, nz)
            z_out[c, d - 1] = (partial[par, j, rows, :] + pair_in[j, rows, :]).astype(bf16)
            z_copy(c, d).start()

    def to_groups(c):
        rows = pl.ds(c * Ec, Ec)
        total = partial[par, zi, rows, :] + pair_in[zi, rows, :]
        for d in range(1, nz):
            z_copy(c, d).wait()
            total = total + z_in[c, d - 1].astype(f32)
        high = total.astype(bf16)
        frag[0, ka, rows, :] = high
        frag[1, ka, rows, :] = (total - high.astype(f32)).astype(bf16)
        for d in range(1, n_ka):
            ka_copy(c, d).start()

    def k_block(p):
        cos_k, sin_k = grid_phases(kn[p * KL : (p + 1) * KL, :])
        kph[p, 0:KL, :] = cos_k.astype(bf16)
        kph[p, KL : 2 * KL, :] = sin_k.astype(bf16)

    for c in range(NC):
        mid_sums(c)
        if c == 0:
            pl.semaphore_wait(barrier, n_rp + n_ka - 2)
        pair_copy(c).start()
        if c >= LAG:
            to_owners(c - LAG)
    for c in range(max(NC - LAG, 0), NC):
        to_owners(c)
    small[2].wait()
    small[3].wait()
    kn[...] = lax.dot_general(
        k_ref[...].astype(f32).astype(bf16), re_ref[...].astype(f32).astype(bf16),
        (((0,), (0,)), ((), ())), preferred_element_type=f32,
    )
    for p in range(n_rp):
        k_block(p)
    for c in range(NC):
        to_groups(c)

    for c in range(NC):
        for d in range(1, n_ka):
            src = frag.at[:, lax.rem(ka + n_ka - d, n_ka), pl.ds(c * Ec, Ec), :]
            ka_copy(c, d).wait_send()
            pltpu.make_async_remote_copy(
                src_ref=src, dst_ref=src,
                send_sem=ka_s.at[c, d - 1], recv_sem=ka_r.at[c, d - 1],
                device_id={"ka": lax.rem(ka + d, n_ka)}, device_id_type=MESH,
            ).wait_recv()

    def coupling(dest):
        ph = kph[dest]
        mid = frag[...].reshape(2, n_ka * E, 2 * C)
        s = jnp.dot(ph, mid[0], preferred_element_type=f32)
        s = s + jnp.dot(ph, mid[1], preferred_element_type=f32)
        real = s[:KL, :C] - s[KL:, C:]
        imag = s[KL:, :C] + s[:KL, C:]
        return jnp.concatenate([real, imag], axis=1)

    for d in range(1, n_rp):
        out_send[d - 1] = coupling(lax.rem(me + d, n_rp)).astype(bf16)
        out_copy(d).start()
    own[...] = coupling(me)

    for d in range(1, n_rp):
        out_copy(d).wait()
    for s in range(n_rp):
        lo, hi = s * C, Q * M + s * C

        @pl.when(me == s)
        def _():
            out_ref[:, lo : lo + C] = own[:, :C]
            out_ref[:, hi : hi + C] = own[:, C:]

        @pl.when(me != s)
        def _():
            block = out_in[lax.rem(me - s + n_rp, n_rp) - 1].astype(f32)
            out_ref[:, lo : lo + C] = block[:, :C]
            out_ref[:, hi : hi + C] = block[:, C:]


def per_device(mesh, coupling_table, k_points, re_vectors, rp_vectors, q_points):
    n_ka, n_rp = mesh.shape["ka"], mesh.shape["rp"]
    E, R, width = coupling_table.shape
    M, Q = width // 2, q_points.shape[1]
    kt = k_points.shape[1]
    KL = kt // n_rp
    nz, C = n_rp // 2, Q * M // n_rp
    Ec = min(CHUNK, E)
    NC = E // Ec
    f32, bf16 = jnp.float32, jnp.bfloat16
    dma = pltpu.SemaphoreType.DMA
    vmem = pl.BlockSpec(memory_space=pltpu.VMEM)
    return pl.pallas_call(
        functools.partial(kernel, (n_ka, n_rp, E, R, M, Q, KL)),
        out_shape=jax.ShapeDtypeStruct((KL, 2 * Q * M), f32),
        in_specs=[pl.BlockSpec(memory_space=pltpu.HBM)] * 5,
        out_specs=vmem,
        scratch_shapes=[
            pltpu.VMEM((Q, 3), jnp.int32),
            pltpu.VMEM(k_points.shape, jnp.int32),
            pltpu.VMEM(re_vectors.shape, jnp.int32),
            pltpu.VMEM(rp_vectors.shape, jnp.int32),
            pltpu.VMEM((E * R, width), bf16),
            pltpu.VMEM((4 * Q * GROUP, GROUP * R), bf16),
            pltpu.VMEM((2, nz, E, 2 * C), f32),
            pltpu.VMEM((nz, E, 2 * C), f32),
            pltpu.VMEM((NC, nz - 1, Ec, 2 * C), bf16),
            pltpu.VMEM((NC, nz - 1, Ec, 2 * C), bf16),
            pltpu.VMEM((2, n_ka, E, 2 * C), bf16),
            pltpu.VMEM((kt, n_ka * E), f32),
            pltpu.VMEM((n_rp, 2 * KL, n_ka * E), bf16),
            pltpu.VMEM((KL, 2 * C), f32),
            pltpu.VMEM((n_rp - 1, KL, 2 * C), bf16),
            pltpu.VMEM((n_rp - 1, KL, 2 * C), bf16),
            dma((4,)), dma((NC,)), dma((NC,)), dma((NC,)), dma((NC, nz - 1)), dma((NC, nz - 1)),
            dma((NC, n_ka - 1)), dma((NC, n_ka - 1)), dma((n_rp - 1,)), dma((n_rp - 1,)),
        ],
        compiler_params=pltpu.CompilerParams(
            collective_id=0, has_side_effects=True, vmem_limit_bytes=67043328
        ),
        name="interpolate",
    )(q_points.T, k_points, re_vectors, rp_vectors, coupling_table.reshape(E * R, width))


def solution(mesh):
    placed = (P("ka", "rp", None), P(None, "ka"), P(), P(None, "rp"), P())
    return jax.shard_map(
        functools.partial(per_device, mesh), mesh=mesh, in_specs=placed,
        out_specs=P(("ka", "rp"), None), check_vma=False,
    )
```
